256 devices in a mesh: aux: 4 (over y), occ: 64 (over z, x, core).
Axes of the slice: x: 4, y: 4, z: 8, core: 2. Of those that a mesh axis runs over, the one named last changes fastest.
Arguments:
- amplitudes: bfloat16 [256, 512, 1024], P('aux', 'occ'), may hold values from -6 to 6
- virtual_orbitals: bfloat16 [1536, 1024], P('aux'), may hold values from -0.1875 to 0.1875
- occupied_orbitals: bfloat16 [1536, 512], P('aux'), may hold values from -0.25 to 0.25
- screening: int32 [12, 12], replicated, may hold values from 0 to 1, as said below
- pair_owner: int32 [12, 12], replicated, may hold values from 0 to 63, as said below
- pair_weight: bfloat16 [128, 128, 128], P('occ'), may hold values from 0.5 to 2
Outputs:
- owned_density: bfloat16 [256, 128, 128, 128], P('aux', 'occ')
The draws below stay inside these ranges and needn't reach their ends.
Inputs may be any that keep to these rules, and one draw needn't show every extreme that they name: `screening`: Symmetric; exactly 58 blocks (r, c) with r <= c are 1. `pair_owner`: Symmetric. Among kept blocks with r <= c, no owner holds more than 2, and some owner holds exactly 2.
All inputs are finite; a program needn't handle non-finite values.
Results may differ from the reference program's by a relative error of at most 0.0085.
Values may be sent and summed in bfloat16 or wider, within the bound.
No kernel may reach another device: no remote copies, remote signals or barrier semaphores. Data moves between devices by JAX's collectives and lax.ppermute only.
A program may use at most 64 MiB of HBM per device.

```python
import math
import jax
import jax.numpy as jnp
from jax import lax

NOCC = 512
NVIR = 1024
NBAS = 1536
BLK = 128
MAXP = 2
NAUX = 256
NB = 12
SLOTS = 128
KEPT = 58
N_OCC = 64


def screen_plan(key):
    key_pairs = jax.random.fold_in(key, 101)
    key_owner = jax.random.fold_in(key, 202)
    key_slots = jax.random.fold_in(key, 303)
    key_rest = jax.random.fold_in(key, 404)
    count = NB * NB
    block_ids = jnp.arange(count, dtype=jnp.int32)
    first = block_ids // NB
    second = block_ids % NB
    canonical = first <= second
    shuffled = jax.random.permutation(key_pairs, count).astype(jnp.int32)
    scores = jnp.where(canonical, shuffled, count + shuffled)
    order = jnp.argsort(scores, stable=True).astype(jnp.int32)
    kept_ids = order[:KEPT]
    busiest = jax.random.randint(key_owner, (), 0, N_OCC).astype(jnp.int32)
    slot_ids = jnp.arange(SLOTS, dtype=jnp.int32)
    slot_shuffle = jax.random.permutation(key_slots, SLOTS).astype(jnp.int32)
    slot_scores = jnp.where(slot_ids // MAXP == busiest, slot_ids % MAXP - MAXP, slot_shuffle)
    slot_order = jnp.argsort(slot_scores, stable=True).astype(jnp.int32)
    kept_owners = slot_order[:KEPT] // MAXP
    base = jax.random.randint(key_rest, (count,), 0, N_OCC).astype(jnp.int32)
    owner_flat = base.at[kept_ids].set(kept_owners)
    mask_flat = jnp.zeros((count,), jnp.int32).at[kept_ids].set(1)
    upper = (first <= second).reshape(NB, NB)
    owner_grid = owner_flat.reshape(NB, NB)
    mask_grid = mask_flat.reshape(NB, NB)
    owner_grid = jnp.where(upper, owner_grid, owner_grid.T)
    mask_grid = jnp.where(upper, mask_grid, mask_grid.T)
    return (mask_grid.astype(jnp.int32), owner_grid.astype(jnp.int32))


def draw_screening(key, part):
    return screen_plan(key)[0]


def draw_pair_owner(key, part):
    return screen_plan(key)[1]


def shard_levels(key, dims, pieces, smallest, top_value):
    def one(axis_at, shards_of):
        steps = jax.random.uniform(jax.random.fold_in(jax.random.fold_in(key, 6), axis_at), (shards_of,), jnp.float32, smallest / len(pieces), top_value / len(pieces))
        return jnp.repeat(jnp.exp(steps), dims[axis_at] // shards_of).reshape((-1,) + (1,) * (len(dims) - axis_at - 1))

    level = one(*pieces[0])
    for cut in pieces[1:]:
        level = level * one(*cut)
    return level


def normal_values(rng, extent, spread, limit, pieces=(), kind=jnp.bfloat16):
    entries = jax.random.normal(rng, extent, jnp.float32) * spread
    if len(pieces) > 0:
        entries = shard_levels(rng, extent, pieces, -0.22, 0.18) * entries
    return jnp.clip(entries, min=-limit, max=limit).astype(kind)


def setup_inputs(seed: int = 0) -> dict:
    streams_of = jax.random.split(jax.random.key(seed), 7)
    amplitudes = normal_values(streams_of[0], (NAUX, NOCC, NVIR), 1.0, 6.0, ((0, 4), (1, 64)))
    virtual_orbitals = normal_values(streams_of[1], (NBAS, NVIR), NVIR ** -0.5, 0.1875, ((0, 4),))
    occupied_orbitals = normal_values(streams_of[2], (NBAS, NOCC), NOCC ** -0.5, 0.25, ((0, 4),))
    screening = draw_screening(jax.random.fold_in(streams_of[6], 71), 0)
    pair_owner = draw_pair_owner(jax.random.fold_in(streams_of[6], 71), 0)
    pair_weight = jnp.clip(jnp.exp(math.log(2.0) - 1.3862944 * jax.random.uniform(streams_of[5], (SLOTS, BLK, BLK), jnp.float32) ** shard_levels(streams_of[5], (SLOTS, BLK, BLK), ((0, 64),), -0.2, 0.2)), 0.5, 2.0).astype(jnp.bfloat16)
    return dict(amplitudes=amplitudes, virtual_orbitals=virtual_orbitals, occupied_orbitals=occupied_orbitals, screening=screening, pair_owner=pair_owner, pair_weight=pair_weight)


def slot_table(screening, pair_owner, slots):
    nblocks = screening.shape[0]
    count = nblocks * nblocks
    block_ids = jnp.arange(count, dtype=jnp.int32)
    first = block_ids // nblocks
    second = block_ids % nblocks
    keep_flag = (screening.reshape(count) == 1) & (first <= second)
    owner_flat = pair_owner.reshape(count)
    earlier = (owner_flat[:, None] == owner_flat[None, :]) & keep_flag[None, :] & (block_ids[None, :] < block_ids[:, None])
    ranks = jnp.sum(earlier.astype(jnp.int32), axis=1).astype(jnp.int32)
    target = jnp.where(keep_flag, owner_flat * MAXP + ranks, -1).astype(jnp.int32)
    matches = target[None, :] == jnp.arange(slots, dtype=jnp.int32)[:, None]
    filled = jnp.any(matches, axis=1)
    chosen = jnp.sum(jnp.where(matches, block_ids[None, :], 0), axis=1).astype(jnp.int32)
    return filled, chosen // nblocks, chosen % nblocks


def reference(amplitudes, virtual_orbitals, occupied_orbitals, screening, pair_owner, pair_weight):
    filled, row_blocks, col_blocks = slot_table(screening, pair_owner, MAXP * N_OCC)
    weights = pair_weight.astype(jnp.float32)

    def one_function(amplitude):
        half = jnp.dot(amplitude, virtual_orbitals.T, preferred_element_type=jnp.float32).astype(jnp.bfloat16)
        full = jnp.dot(occupied_orbitals, half, preferred_element_type=jnp.float32).astype(jnp.bfloat16)
        nblocks = screening.shape[0]
        grid = full.reshape(nblocks, BLK, nblocks, BLK)
        direct = grid[row_blocks, :, col_blocks, :]
        mirror = grid[col_blocks, :, row_blocks, :]
        folded = (direct.astype(jnp.float32) + jnp.swapaxes(mirror, -1, -2).astype(jnp.float32)).astype(jnp.bfloat16)
        folded = jnp.where(filled[:, None, None], folded, jnp.zeros_like(folded))
        return (weights * folded.astype(jnp.float32)).astype(jnp.bfloat16)

    return lax.map(one_function, amplitudes)
```

```python
import functools

import jax
import jax.numpy as jnp
from jax import lax
from jax.experimental import pallas as pl
from jax.experimental.pallas import tpu as pltpu
from jax.sharding import Mesh
from jax.sharding import PartitionSpec as P

MAXP = 2
BLK = 128
ROW = ("x", "core")
SIZES = (2, 2, 2, 2)


def slot_table(screening, pair_owner, first_slot, slots):
    nblocks = screening.shape[0]
    count = nblocks * nblocks
    block_ids = jnp.arange(count, dtype=jnp.int32)
    keep_flag = (screening.reshape(count) == 1) & (block_ids // nblocks <= block_ids % nblocks)
    owner_flat = pair_owner.reshape(count)
    earlier = (
        (owner_flat[:, None] == owner_flat[None, :])
        & keep_flag[None, :]
        & (block_ids[None, :] < block_ids[:, None])
    )
    ranks = jnp.sum(earlier.astype(jnp.int32), axis=1)
    target = jnp.where(keep_flag, owner_flat * MAXP + ranks, -1)
    wanted = first_slot + jnp.arange(slots, dtype=jnp.int32)
    matches = target[None, :] == wanted[:, None]
    return jnp.sum(jnp.where(matches, block_ids[None, :] + 1, 0), axis=1)


def transform_kernel(count, nb, table, place, *refs):
    own, f1, f2, f3, f4, b1, b2, b3, b4, coef, out, amp, half = refs
    z = place[0]
    width = own.shape[1]
    rows = 8 * width
    nvir = own.shape[2]

    def spot(step):
        return pl.multiple_of(lax.rem(z + step, 8) * width, width)

    for p in range(count):
        for step, slab in ((0, own), (1, b1), (2, b2), (3, b3), (5, f3), (6, f2), (7, f1)):
            amp[p, pl.ds(spot(step), width), :] = slab[p]
        far = spot(4)
        amp[p, pl.ds(far, width // 2), :] = f4[p]
        amp[p, pl.ds(pl.multiple_of(far + width // 2, width // 2), width // 2), :] = b4[p]
    for p in range(count):
        for c in range(0, nb, 2):
            product = lax.dot_general(
                amp[p],
                coef[c * BLK : (c + 2) * BLK, :nvir],
                (((1,), (1,)), ((), ())),
                preferred_element_type=jnp.float32,
            ).astype(jnp.bfloat16)
            half[p, c] = product[:, :BLK]
            half[p, c + 1] = product[:, BLK:]

    def one_slot(s, carry):
        entry = table[s]
        dest, rank = s // MAXP, lax.rem(s, MAXP)

        @pl.when(entry == 0)
        def _():
            for p in range(count):
                out[dest, p, rank] = jnp.zeros((BLK, BLK), jnp.bfloat16)

        @pl.when(entry > 0)
        def _():
            r, c = (entry - 1) // nb, lax.rem(entry - 1, nb)
            row_coef = coef[pl.ds(pl.multiple_of(r * BLK, BLK), BLK), nvir:]
            col_coef = coef[pl.ds(pl.multiple_of(c * BLK, BLK), BLK), nvir:]
            for p in range(count):
                direct = jnp.dot(row_coef, half[p, c], preferred_element_type=jnp.float32)
                mirror = jnp.dot(col_coef, half[p, r], preferred_element_type=jnp.float32)
                direct = direct.astype(jnp.bfloat16).astype(jnp.float32)
                mirror = mirror.astype(jnp.bfloat16).astype(jnp.float32)
                out[dest, p, rank] = (direct + mirror.T).astype(jnp.bfloat16)

        return carry

    lax.fori_loop(0, table.shape[0], one_slot, 0)


def transform(table, place, slabs, coef):
    count, width, nvir = slabs[0].shape
    nb = coef.shape[0] // BLK
    slots = table.shape[0]
    vmem = pl.BlockSpec(memory_space=pltpu.VMEM)
    smem = pl.BlockSpec(memory_space=pltpu.SMEM)
    return pl.pallas_call(
        functools.partial(transform_kernel, count, nb),
        out_shape=jax.ShapeDtypeStruct((slots // MAXP, count, MAXP, BLK, BLK), jnp.bfloat16),
        in_specs=[smem, smem] + [vmem] * 10,
        out_specs=vmem,
        scratch_shapes=[
            pltpu.VMEM((count, 8 * width, nvir), jnp.bfloat16),
            pltpu.VMEM((count, nb, 8 * width, BLK), jnp.bfloat16),
        ],
        cost_estimate=pl.CostEstimate(
            flops=count * 2 * 8 * width * nvir * nb * BLK, bytes_accessed=count * 2_000_000 + 4_700_000, transcendentals=0
        ),
        name="transform",
    )(table, place, *slabs, coef)


def weigh_kernel(*refs):
    weight, block, out = refs[0], refs[1], refs[-1]
    out[...] = (weight[...].astype(jnp.float32)[None] * block[...].astype(jnp.float32)).astype(jnp.bfloat16)


def weigh(weight, blocks, total, first, previous):
    step = 8
    base = first // step
    in_specs = [
        pl.BlockSpec(weight.shape, lambda g: (0, 0, 0)),
        pl.BlockSpec((step, MAXP, BLK, BLK), lambda g: (g, 0, 0, 0)),
    ]
    args, aliases = [weight, blocks], {}
    if previous is not None:
        in_specs.append(pl.BlockSpec(memory_space=pl.ANY))
        args.append(previous)
        aliases = {2: 0}
    return pl.pallas_call(
        weigh_kernel,
        grid=(blocks.shape[0] // step,),
        out_shape=jax.ShapeDtypeStruct((total, MAXP, BLK, BLK), jnp.bfloat16),
        in_specs=in_specs,
        out_specs=pl.BlockSpec((step, MAXP, BLK, BLK), lambda g: (base + g, 0, 0, 0)),
        input_output_aliases=aliases,
        cost_estimate=pl.CostEstimate(flops=blocks.size, bytes_accessed=4 * blocks.size, transcendentals=0),
        name="weigh",
    )(*args)


def ring(size, step):
    return [(i, (i + step) % size) for i in range(size)]


def gather_coefficients(virtual_orbitals, occupied_orbitals):
    core, y = lax.axis_index("core"), lax.axis_index("aux")
    packed = jnp.concatenate([virtual_orbitals, occupied_orbitals], axis=1)
    rows = packed.shape[0] // 2
    mine = lax.dynamic_slice_in_dim(packed, core * rows, rows, 0)
    up, down = ring(4, 1), ring(4, -1)
    f1 = lax.ppermute(mine, "aux", up)
    b1 = lax.ppermute(mine, "aux", down)
    f2 = lax.ppermute(f1[: rows // 2], "aux", up)
    b2 = lax.ppermute(b1[rows // 2 :], "aux", down)
    own = jnp.zeros((4, rows, packed.shape[1]), jnp.bfloat16)
    for step, part, at in ((0, mine, 0), (3, f1, 0), (1, b1, 0), (2, f2, 0), (2, b2, rows // 2)):
        own = lax.dynamic_update_slice(own, part[None], ((y + step) % 4, at, 0))
    other = lax.ppermute(own, "core", [(0, 1), (1, 0)])
    both = jnp.zeros((4, 2, rows, packed.shape[1]), jnp.bfloat16)
    both = lax.dynamic_update_slice(both, own[:, None], (0, core, 0, 0))
    both = lax.dynamic_update_slice(both, other[:, None], (0, 1 - core, 0, 0))
    return both.reshape(8 * rows, packed.shape[1])


def circulate(own, after):
    up, down = ring(8, 1), ring(8, -1)
    if after is not None:
        own, _ = lax.optimization_barrier((own, after))
    f1, b1 = lax.ppermute(own, "z", up), lax.ppermute(own, "z", down)
    f2, b2 = lax.ppermute(f1, "z", up), lax.ppermute(b1, "z", down)
    f3, b3 = lax.ppermute(f2, "z", up), lax.ppermute(b2, "z", down)
    split = own.shape[1] // 2
    f4, b4 = lax.ppermute(f3[:, :split], "z", up), lax.ppermute(b3[:, split:], "z", down)
    return (own, f1, f2, f3, f4, b1, b2, b3, b4), (f2, b2)


def per_device(amplitudes, virtual_orbitals, occupied_orbitals, screening, pair_owner, pair_weight):
    functions = amplitudes.shape[0]
    z = lax.axis_index("z").astype(jnp.int32)
    row_slots = 8 * MAXP
    chunks, first = [], 0
    for size in SIZES:
        part = lax.slice_in_dim(amplitudes, first, first + 8 * size, axis=0)
        chunks.append((first, lax.all_to_all(part, ROW, split_axis=0, concat_axis=1, tiled=True)))
        first += 8 * size
    coef = gather_coefficients(virtual_orbitals, occupied_orbitals)
    table = slot_table(screening, pair_owner, z * row_slots, row_slots)
    place = z.reshape(1)
    result, after = None, None
    for first, own in chunks:
        slabs, after = circulate(own, after)
        blocks = transform(table, place, slabs, coef)
        moved = lax.all_to_all(blocks, ROW, split_axis=0, concat_axis=0, tiled=True)
        moved = moved.reshape(-1, MAXP, BLK, BLK)
        result = weigh(pair_weight, moved, functions, first, result)
    return result


def solution(mesh):
    full = Mesh(mesh.devices.reshape(4, 8, 4, 2), ("aux", "z", "x", "core"))
    occ = ("z", "x", "core")
    return jax.shard_map(
        per_device,
        mesh=full,
        in_specs=(P("aux", occ, None), P("aux", None), P("aux", None), P(), P(), P(occ, None, None)),
        out_specs=P("aux", occ, None, None),
        check_vma=False,
    )
```

```python
import functools

import jax
import jax.numpy as jnp
from jax import lax
from jax.experimental import pallas as pl
from jax.experimental.pallas import tpu as pltpu
from jax.sharding import Mesh
from jax.sharding import PartitionSpec as P


MAXP = 2
BLK = 128
ROW = ("x", "core")
GROUPS = ((2, 2, 2, 2),)

ANY = pl.BlockSpec(memory_space=pl.ANY)
HBM = pl.BlockSpec(memory_space=pltpu.HBM)
SMEM = pl.BlockSpec(memory_space=pltpu.SMEM)
VMEM = pl.BlockSpec(memory_space=pltpu.VMEM)


def slot_table(screening, pair_owner, first_slot, slots):
    nblocks = screening.shape[0]
    count = nblocks * nblocks
    block_ids = jnp.arange(count, dtype=jnp.int32)
    keep_flag = (screening.reshape(count) == 1) & (block_ids // nblocks <= block_ids % nblocks)
    owner_flat = pair_owner.reshape(count)
    earlier = (
        (owner_flat[:, None] == owner_flat[None, :])
        & keep_flag[None, :]
        & (block_ids[None, :] < block_ids[:, None])
    )
    ranks = jnp.sum(earlier.astype(jnp.int32), axis=1)
    target = jnp.where(keep_flag, owner_flat * MAXP + ranks, -1)
    wanted = first_slot + jnp.arange(slots, dtype=jnp.int32)
    matches = target[None, :] == wanted[:, None]
    return jnp.sum(jnp.where(matches, block_ids[None, :] + 1, 0), axis=1)


def compact(present, items, count):
    def one(k, found):
        there = present(k)

        @pl.when(there)
        def _():
            items[found] = k

        return found + there.astype(jnp.int32)

    return lax.fori_loop(0, count, one, jnp.int32(0))


def transform_kernel(count, nb, table, place, *refs):
    own, m1, m2, m3, s1, s2, s3, far, virt_in, occ_in, out = refs[:11]
    amp, virt, occ, half, stage, filled, slab_sem, virt_sem, occ_sem, out_sem = refs[11:]
    z, core = place[0], place[2]
    width = own.shape[1]
    slots = table.shape[0]
    unroll = 4

    def slab_copy(k, slab, first, step):
        row = lax.rem(z + jnp.where(core == 0, 8 - step, 8 + step), 8)
        at = pl.ds(pl.multiple_of(row * width, width), width)
        return pltpu.make_async_copy(slab.at[pl.ds(first, count)], amp.at[:, at, :], slab_sem.at[k])

    moved = [(m1, 0, 1), (m2, 0, 2), (m3, 0, 3), (s1, count, -1), (s2, count, -2), (s3, count, -3)]
    parts = [(own, 0, 0), *moved, (far, 0, 4)]
    slab_copies = [slab_copy(k, *part) for k, part in enumerate(parts)]
    for copy in slab_copies:
        copy.start()

    def virt_copy(k):
        return pltpu.make_async_copy(virt_in.at[k], virt.at[k], virt_sem.at[k])

    def out_copy(s):
        return pltpu.make_async_copy(stage.at[s], out.at[s // MAXP, :, lax.rem(s, MAXP)], out_sem.at[s])

    occ_copy = pltpu.make_async_copy(occ_in, occ, occ_sem)
    virt_copy(0).start()
    busy = compact(lambda s: table[s] > 0, filled, slots)

    def empty(s, carry):
        @pl.when(table[s] == 0)
        def _():
            stage[s] = jnp.zeros(stage.shape[1:], stage.dtype)
            out_copy(s).start()

        return carry

    lax.fori_loop(0, slots, empty, 0)
    for copy in slab_copies:
        copy.wait()
    for k in range(1, virt.shape[0]):
        virt_copy(k).start()
    occ_copy.start()
    wide = virt.shape[2] // BLK

    def some_columns(k, carry):
        virt_copy(k).wait()
        for p in range(count):
            product = jnp.dot(amp[p], virt[k], preferred_element_type=jnp.float32).astype(jnp.bfloat16)
            for j in range(wide):
                half[wide * k + j, :, p * BLK : (p + 1) * BLK] = product[:, j * BLK : (j + 1) * BLK]
        return carry

    lax.fori_loop(0, virt.shape[0], some_columns, 0)
    occ_copy.wait()

    def product_of(block_row, block_col):
        return jnp.dot(occ[block_row], half[block_col], preferred_element_type=jnp.float32).astype(jnp.bfloat16)

    def some_slots(k, carry):
        group = [filled[jnp.minimum(unroll * k + j, busy - 1)] for j in range(unroll)]
        ends = [((table[s] - 1) // nb, lax.rem(table[s] - 1, nb)) for s in group]
        found = [(product_of(r, c), product_of(c, r)) for r, c in ends]
        for s, (direct, mirror) in zip(group, found):
            for p in range(count):
                span = slice(p * BLK, (p + 1) * BLK)
                total = direct[:, span].astype(jnp.float32) + mirror[:, span].T.astype(jnp.float32)
                stage[s, p] = total.astype(jnp.bfloat16)
        for j, s in enumerate(group):

            @pl.when(unroll * k + j < busy)
            def _():
                out_copy(s).start()

        return carry

    lax.fori_loop(0, (busy + unroll - 1) // unroll, some_slots, 0)

    def end(s, carry):
        out_copy(s).wait()
        return carry

    lax.fori_loop(0, slots, end, 0)


def transform(table, place, slabs, virt, occ):
    count, width, nvir = slabs[0].shape
    nocc = 8 * width
    nb = occ.shape[0]
    slots = table.shape[0]
    dma = pltpu.SemaphoreType.DMA
    return pl.pallas_call(
        functools.partial(transform_kernel, count, nb),
        out_shape=jax.ShapeDtypeStruct((slots // MAXP, count, MAXP, BLK, BLK), jnp.bfloat16),
        in_specs=[SMEM, SMEM] + [ANY] * 10,
        out_specs=ANY,
        scratch_shapes=[
            pltpu.VMEM((count, nocc, nvir), jnp.bfloat16),
            pltpu.VMEM(virt.shape, jnp.bfloat16),
            pltpu.VMEM(occ.shape, jnp.bfloat16),
            pltpu.VMEM((nb, nocc, count * BLK), jnp.bfloat16),
            pltpu.VMEM((slots, count, BLK, BLK), jnp.bfloat16),
            pltpu.SMEM((slots,), jnp.int32),
            dma((8,)),
            dma((virt.shape[0],)),
            dma(()),
            dma((slots,)),
        ],
        cost_estimate=pl.CostEstimate(
            flops=count * 2 * nocc * nvir * nb * BLK, bytes_accessed=count * 2_000_000 + 4_700_000, transcendentals=0
        ),
        compiler_params=pltpu.CompilerParams(vmem_limit_bytes=24 << 20),
        name="transform",
    )(table, place, *slabs, virt, occ)


def pack_kernel(virt, occ, out):
    rows, nvir = virt.shape
    out[:nvir, :] = virt[...].T
    for k in range(occ.shape[1] // BLK):
        for j in range(rows // BLK):
            block = occ[j * BLK : (j + 1) * BLK, k * BLK : (k + 1) * BLK]
            out[nvir + k * BLK : nvir + (k + 1) * BLK, j * BLK : (j + 1) * BLK] = block


def pack(virtual_orbitals, occupied_orbitals):
    rows, nvir = virtual_orbitals.shape
    nocc = occupied_orbitals.shape[1]
    return pl.pallas_call(
        pack_kernel,
        out_shape=jax.ShapeDtypeStruct((nvir + nocc, rows), jnp.bfloat16),
        in_specs=[VMEM, VMEM],
        out_specs=VMEM,
        cost_estimate=pl.CostEstimate(flops=0, bytes_accessed=3_500_000, transcendentals=0),
        name="pack",
    )(virtual_orbitals, occupied_orbitals)


def assemble_kernel(nvir, place, *refs):
    pieces, (virt, occ) = refs[:5], refs[5:]
    y, core = place[1], place[2]
    wide = virt.shape[2] // BLK
    per_shard = occ.shape[0] // 4
    middle = pieces[0].shape[0] // 2

    def put(ref, start, step):
        first = lax.rem(y + step, 4) * per_shard
        for j in range(per_shard):
            block = first + j
            lanes = slice(j * BLK, (j + 1) * BLK)
            upper = min(ref.shape[0], max(0, nvir - start))
            if upper:
                at = pl.ds(pl.multiple_of(lax.rem(block, wide) * BLK, BLK), BLK)
                virt[block // wide, start : start + upper, at] = ref[:upper, lanes]
            for top in range(upper, ref.shape[0], BLK):
                across = start + top - nvir
                occ[block, :, across : across + BLK] = ref[top : top + BLK, lanes]

    mine, near, half, twin_near, twin_half = pieces
    put(mine, 0, 0)

    @pl.when(core == 0)
    def _():
        put(near, 0, 3)
        put(twin_near, 0, 1)
        put(half, 0, 2)
        put(twin_half, middle, 2)

    @pl.when(core == 1)
    def _():
        put(near, 0, 1)
        put(twin_near, 0, 3)
        put(half, middle, 2)
        put(twin_half, 0, 2)


def gather_coefficients(place, virtual_orbitals, occupied_orbitals, nb):
    nvir, nocc = virtual_orbitals.shape[1], occupied_orbitals.shape[1]
    wide = 4
    mine = pack(virtual_orbitals, occupied_orbitals)
    middle = mine.shape[0] // 2
    near = hop(mine, "aux", 4)
    half = lax.dynamic_slice_in_dim(near, place[2] * middle, middle, axis=0)
    half = hop(half, "aux", 4)
    twin_near = swap(near)
    twin_half = swap(half)
    return pl.pallas_call(
        functools.partial(assemble_kernel, nvir),
        out_shape=(
            jax.ShapeDtypeStruct((nb // wide, nvir, wide * BLK), jnp.bfloat16),
            jax.ShapeDtypeStruct((nb, BLK, nocc), jnp.bfloat16),
        ),
        in_specs=[SMEM] + [VMEM] * 5,
        out_specs=(VMEM, VMEM),
        cost_estimate=pl.CostEstimate(flops=0, bytes_accessed=9_400_000, transcendentals=0),
        name="assemble",
    )(place, mine, near, half, twin_near, twin_half)


def swap(array):
    return lax.ppermute(array, "core", [(0, 1), (1, 0)])


def hop(array, axis, size):
    pairs = [(2 * i, 2 * ((i + 1) % size)) for i in range(size)]
    pairs += [(2 * i + 1, 2 * ((i - 1) % size) + 1) for i in range(size)]
    return lax.ppermute(array, (axis, "core"), pairs)


def blank(shape, dtype):
    def kernel(out):
        del out

    return pl.pallas_call(
        kernel,
        out_shape=jax.ShapeDtypeStruct(shape, dtype),
        out_specs=ANY,
        name="blank",
    )()


def weigh(weight, blocks, at, result):
    weighed = (weight.astype(jnp.float32) * blocks.astype(jnp.float32)).astype(jnp.bfloat16)
    return lax.dynamic_update_slice(result, weighed, (0, at, 0, 0, 0))


def circulate(own):
    size = own.shape[0]
    twin = swap(own)
    moved = [jnp.concatenate([own, twin], axis=0)]
    swapped = []
    for _ in range(3):
        moved.append(hop(moved[-1], "z", 8))
        swapped.append(swap(moved[-1]))
    last = lax.slice_in_dim(moved[-1], 0, size, axis=0)
    far = hop(last, "z", 8)
    return (own, *moved[1:], *swapped, far)


def per_device(amplitudes, virtual_orbitals, occupied_orbitals, screening, pair_owner, pair_weight):
    functions = amplitudes.shape[0]
    nb = screening.shape[0]
    z = lax.axis_index("z").astype(jnp.int32)
    row_slots = 8 * MAXP
    place = jnp.stack([z, lax.axis_index("aux").astype(jnp.int32), lax.axis_index("core").astype(jnp.int32)])
    chunks, first = [], 0
    for group in GROUPS:
        stride = sum(group)
        part = lax.slice_in_dim(amplitudes, first, first + 8 * stride, axis=0)
        part = lax.all_to_all(part, ROW, split_axis=0, concat_axis=1, tiled=True)
        at = 0
        for size in group:
            chunks.append((first + at, stride, lax.slice_in_dim(part, at, at + size, axis=0)))
            at += size
        first += 8 * stride
    virt, occ = gather_coefficients(place, virtual_orbitals, occupied_orbitals, nb)
    table = slot_table(screening, pair_owner, z * row_slots, row_slots)
    result = blank((functions // stride, stride, MAXP, BLK, BLK), jnp.bfloat16)
    for first, stride, own in chunks:
        slabs = circulate(own)
        blocks = transform(table, place, slabs, virt, occ)
        moved = lax.all_to_all(blocks, ROW, split_axis=0, concat_axis=0, tiled=True)
        result = weigh(pair_weight, moved, first, result)
    return result.reshape(functions, MAXP, BLK, BLK)


def solution(mesh):
    full = Mesh(mesh.devices.reshape(4, 8, 4, 2), ("aux", "z", "x", "core"))
    occ = ("z", "x", "core")
    return jax.shard_map(
        per_device,
        mesh=full,
        in_specs=(P("aux", occ, None), P("aux", None), P("aux", None), P(), P(), P(occ, None, None)),
        out_specs=P("aux", occ, None, None),
        check_vma=False,
    )
```
